512 devices in a mesh: gx: 32 (over y, z_lo, core), gy: 16 (over x, z_hi).
Axes of the slice: x: 4, y: 4, z: 16 (z_hi: 4, z_lo: 4; z = z_hi * 4 + z_lo), core: 2. Of those that a mesh axis runs over, the one named last changes fastest.
Arguments:
- tokens: bfloat16 [2, 16, 128, 128, 512], P(None, None, 'gx', 'gy'), may hold values from -6 to 6
- norm_gain: float32 [512], replicated, may hold values from 0.1 to 1.9
- w_qkv: bfloat16 [512, 1536], replicated, may hold values from -12 to 12
- w_out: bfloat16 [512, 512], replicated, may hold values from -1 to 1
Outputs:
- result: bfloat16 [2, 16, 128, 128, 512], P(None, None, 'gx', 'gy')
The draws below stay inside these ranges and needn't reach their ends.
All inputs are finite; a program needn't handle non-finite values.
Results may differ from the reference program's by a relative error of at most 0.0095.
Values may be sent and summed in bfloat16 or wider, within the bound.
A program may use at most 64 MiB of HBM per device.

```python
import jax
import jax.numpy as jnp
from jax import lax

D = 512
HEADS = 8
TSTEPS = 16
BATCH = 2
NX = 128
NY = 128


def draw_w_qkv(key, part):
    primary = jnp.clip(jax.random.normal(jax.random.fold_in(key, 11), (D, 3 * D), jnp.float32), -4.0, 4.0) / jnp.sqrt(jnp.float32(D))
    return primary.astype(jnp.bfloat16)


def shard_levels(key, dims, pieces, least, high):
    factor_of, own = 1.0, jax.random.fold_in(key, 6)
    for axis_at, shards_of in pieces:
        steps = jnp.exp(jax.random.uniform(jax.random.fold_in(own, axis_at), (shards_of,), jnp.float32, least / len(pieces), high / len(pieces)))
        factor_of = factor_of * jnp.repeat(steps, dims[axis_at] // shards_of).reshape([-1 if axis == axis_at else 1 for axis in range(len(dims))])
    return factor_of


def scatter_about(own_key, extent, spread, reach, shards=(), kind=jnp.bfloat16):
    values = spread * jax.random.normal(own_key, extent, jnp.float32)
    if shards:
        values = values * shard_levels(own_key, extent, shards, -0.22, 0.18)
    return jnp.clip(values, -reach, reach).astype(kind)


def setup_inputs(seed: int = 0) -> dict:
    key_list = jax.random.split(jax.random.key(seed), 5)
    return {
        "tokens": scatter_about(key_list[0], (BATCH, TSTEPS, NX, NY, D), 1.0, 6.0, ((2, 32), (3, 16))),
        "norm_gain": jnp.clip(1.0 + 0.18 * jax.random.normal(key_list[1], (D,), jnp.float32), 0.1, 1.9),
        "w_qkv": draw_w_qkv(jax.random.fold_in(key_list[4], 71), 0),
        "w_out": scatter_about(key_list[3], (D, D), (D // 16) ** -0.5, 1.0),
    }


def attend(triple, seq_dim):
    shape = triple.shape
    width = shape[-1] // 3
    head_size = width // HEADS
    split = shape[:-1] + (HEADS, head_size)
    queries = triple[..., :width].reshape(split).astype(jnp.float32)
    key_part = triple[..., width:2 * width].reshape(split).astype(jnp.float32)
    values = triple[..., 2 * width:].reshape(split).astype(jnp.float32)
    if seq_dim == 1:
        form_scores, form_mix = ('asche,atche->achst', 'achst,atche->asche')
    else:
        form_scores, form_mix = ('acshe,acthe->achst', 'achst,acthe->acshe')
    scores = jnp.einsum(form_scores, queries, key_part) / jnp.sqrt(jnp.float32(head_size))
    highest = lax.optimization_barrier(jnp.max(scores, axis=-1, keepdims=True))
    expo = jnp.exp(scores - highest)
    weights = (expo / lax.optimization_barrier(jnp.sum(expo, axis=-1, keepdims=True))).astype(jnp.bfloat16)
    mixed = jnp.einsum(form_mix, weights.astype(jnp.float32), values)
    return mixed.reshape(shape[:-1] + (width,)).astype(jnp.bfloat16)

def reference(tokens, norm_gain, w_qkv, w_out):
    batch, steps, cells_x, cells_y, width = tokens.shape
    field = tokens.astype(jnp.float32)
    normed = (field * lax.rsqrt(lax.optimization_barrier(jnp.mean(field * field, axis=-1, keepdims=True)) + 1e-05) * norm_gain).astype(jnp.bfloat16)
    triple = jnp.dot(normed.reshape(-1, width), w_qkv, preferred_element_type=jnp.float32).astype(jnp.bfloat16)
    triple = triple.reshape(batch, steps, cells_x, cells_y, 3 * width)
    along_time = lax.map(lambda sample: attend(sample.reshape(1, steps, cells_x * cells_y, 3 * width), 1), triple)
    along_time = along_time.reshape(batch, steps, cells_x, cells_y, width)
    flat = triple.reshape(batch * steps, cells_x, cells_y, 3 * width)
    along_x = lax.map(lambda plane: attend(plane[None], 1)[0], flat)
    along_y = lax.map(lambda plane: attend(plane[None], 2)[0], flat)
    mixed = (along_time.astype(jnp.float32) + along_x.reshape(along_time.shape).astype(jnp.float32) + along_y.reshape(along_time.shape).astype(jnp.float32)).astype(jnp.bfloat16)
    update = jnp.dot(mixed.reshape(-1, width), w_out, preferred_element_type=jnp.float32)
    return (field + update.reshape(field.shape)).astype(jnp.bfloat16)
```

```python
import functools

import jax
import jax.numpy as jnp
from jax import lax
from jax.experimental import pallas as pl
from jax.experimental.pallas import tpu as pltpu
from jax.sharding import PartitionSpec as P

NZ = 16
ROWS = 32
D = 512
MESH = pl.DeviceIdType.MESH
BF = jnp.bfloat16
F32 = jnp.float32


def device(y, zl, core, x, zh):
    return ((y * 4 + zl) * 2 + core, x * 4 + zh)


def kernel(
    tok, gain, wq, wo, out,
    t_s, xn, r1, ry, rx, oy, ox, by, bx, sm, h, tm, res, qkv, of, w, wos,
    load_sem, loc_sem, zs, zr, ys, yr, xs, xr, bys, byr, bxs, bxr, rs, rr, out_sem,
):
    gx, gy = lax.axis_index("gx"), lax.axis_index("gy")
    y, zl, core = gx // 8, (gx // 2) % 4, gx % 2
    x, zh = gy // 4, gy % 4
    z = zh * 4 + zl
    yc = y * 2 + core

    loads = [
        pltpu.make_async_copy(tok.at[0], t_s.at[0], load_sem.at[0]),
        pltpu.make_async_copy(tok.at[1], t_s.at[1], load_sem.at[1]),
        pltpu.make_async_copy(wq, w, load_sem.at[2]),
        pltpu.make_async_copy(wo, wos, load_sem.at[3]),
    ]
    for copy in loads:
        copy.start()

    barrier = pltpu.get_barrier_semaphore()

    def z_peer(i):
        other = (z + i) % NZ
        return other, device(y, other % 4, core, x, other // 4)

    def x_peer(i):
        other = (x + i) % 4
        return other, device(y, zl, core, other, zh)

    def yc_peer(i):
        other = (yc + i) % 8
        return other, device(other // 2, zl, other % 2, x, zh)

    def greet(peer):
        def step(i, carry):
            pl.semaphore_signal(barrier, inc=1, device_id=peer(i)[1], device_id_type=MESH)
            return carry

        return step

    lax.fori_loop(1, NZ, greet(z_peer), 0)
    lax.fori_loop(1, 4, greet(x_peer), 0)
    lax.fori_loop(1, 8, greet(yc_peer), 0)

    scale = gain[...]

    def normalize(b):
        def step(i, carry):
            field = t_s[b, i].astype(F32)
            mean = jnp.mean(field * field, axis=-1, keepdims=True)
            xn[b, i] = (field * lax.rsqrt(mean + 1e-05) * scale).astype(BF)
            return carry

        lax.fori_loop(0, NZ, step, 0)

    def send(src, dst, ssem, rsem, peer):
        pltpu.make_async_remote_copy(
            src_ref=src, dst_ref=dst, send_sem=ssem, recv_sem=rsem, device_id=peer, device_id_type=MESH
        ).start()

    def arrived(ref, sem):
        pltpu.make_async_copy(ref, ref, sem).wait()

    def forward(b):
        own = pltpu.make_async_copy(xn.at[b, z], r1.at[b, zh, zl], loc_sem.at[b, 0])
        own.start()

        def step(i, carry):
            other, peer = z_peer(i)
            send(xn.at[b, other], r1.at[b, zh, zl], zs.at[b], zr.at[b], peer)
            return carry

        lax.fori_loop(1, NZ, step, 0)

    def spread(b):
        arrived(xn.at[b, pl.ds(0, NZ - 1)], zr.at[b])
        pltpu.make_async_copy(xn.at[b, z], r1.at[b, zh, zl], loc_sem.at[b, 0]).wait()
        own = pltpu.make_async_copy(r1.at[b, :, x], ry.at[b, x], loc_sem.at[b, 1])
        own.start()

        def step(i, carry):
            other, peer = x_peer(i)
            send(r1.at[b, :, other], ry.at[b, x], ys.at[b], yr.at[b], peer)
            return carry

        lax.fori_loop(1, 4, step, 0)

        @pl.when(core == b)
        def _():
            pltpu.make_async_copy(r1.at[b, y], rx.at[yc], loc_sem.at[b, 2]).start()

        def step_x(i, carry):
            other = (y + i) % 4

            @pl.when((other != y) | (core != b))
            def _():
                send(r1.at[b, other], rx.at[yc], xs.at[b], xr.at[b], device(other, zl, b, x, zh))

            return carry

        lax.fori_loop(0, 4, step_x, 0)

    def project(src, rows):
        def step(i, carry):
            at = pl.multiple_of(i * 256, 256)
            part = jnp.dot(src[...].reshape(rows, D), w[:, pl.ds(at, 256)], preferred_element_type=F32)
            qkv[2 * i, pl.ds(0, rows)] = part[:, :128]
            qkv[2 * i + 1, pl.ds(0, rows)] = part[:, 128:]
            return carry

        lax.fori_loop(0, 6, step, 0)

    low = lax.broadcasted_iota(jnp.int32, (128, 128), 1) < 64
    ones = jnp.ones((128, 128), BF)

    def line(load, store, mask):
        for pair in range(4):
            q = load(pair) * 0.125
            k = load(4 + pair).astype(BF)
            v = load(8 + pair).astype(BF)
            both = jnp.concatenate([jnp.where(low, q, 0.0), jnp.where(low, 0.0, q)], axis=0).astype(BF)
            scores = lax.dot_general(both, k, (((1,), (1,)), ((), ())), preferred_element_type=F32)
            if mask is not None:
                scores = jnp.where(mask, scores, -3e38)
            weights = jnp.exp(scores - jnp.max(scores, axis=-1, keepdims=True)).astype(BF)
            total = jnp.dot(weights, jnp.concatenate([v, ones], axis=1), preferred_element_type=F32)
            part = jnp.where(low, total[:128, :128], total[128:, :128])
            norm = jnp.where(low, total[:128, 128:], total[128:, 128:])
            store(pair, part / norm)

    def aligned_lines(mask):
        def step(c, carry):
            def rows(g):
                return pl.ds(pl.multiple_of(g * ROWS + c * 8, 8), 8)

            def load(col):
                return jnp.concatenate([qkv[col, rows(g)] for g in range(16)], axis=0)

            def store(col, value):
                for g in range(16):
                    of[col, rows(g)] = value[8 * g : 8 * g + 8]

            line(load, store, mask)
            return carry

        lax.fori_loop(0, 4, step, 0)

    def strided_lines():
        def step(c, carry):
            def load(col):
                return qkv[col, pl.ds(c, 128, stride=8)]

            def store(col, value):
                of[col, pl.ds(c, 128, stride=8)] = value

            line(load, store, None)
            return carry

        lax.fori_loop(0, 8, step, 0)

    def rounded(dst, lead):
        def step(i, carry):
            at = pl.multiple_of(i * 128, 128)
            whole = jnp.concatenate([of[pair, pl.ds(at, 128)] for pair in range(4)], axis=1)
            dst[i] = whole.reshape(4, ROWS, D).astype(BF)
            return carry

        lax.fori_loop(0, lead, step, 0)

    row = lax.broadcasted_iota(jnp.int32, (256, 128), 0)
    column = lax.broadcasted_iota(jnp.int32, (256, 128), 1)
    same_cell = (row % 8) == (column % 8)

    def time_lines(b):
        project(xn.at[b], 512)
        aligned_lines(same_cell)
        rounded(tm.at[b], 4)

    def y_lines(b):
        arrived(ry.at[b, pl.ds(0, 3)], yr.at[b])
        pltpu.make_async_copy(r1.at[b, :, x], ry.at[b, x], loc_sem.at[b, 1]).wait()
        project(ry.at[b], 512)
        aligned_lines(None)
        rounded(oy.at[b], 4)
        pltpu.make_async_copy(oy.at[b, x], by.at[b, x], loc_sem.at[b, 3]).start()

        def step(i, carry):
            other, peer = x_peer(i)
            send(oy.at[b, other], by.at[b, x], bys.at[b], byr.at[b], peer)
            return carry

        lax.fori_loop(1, 4, step, 0)

    def x_lines(b):
        @pl.when(core == b)
        def _():
            arrived(rx.at[pl.ds(0, 7)], xr.at[b])
            pltpu.make_async_copy(r1.at[b, y], rx.at[yc], loc_sem.at[b, 2]).wait()
            project(rx, 1024)
            strided_lines()
            rounded(ox, 8)
            pltpu.make_async_copy(ox.at[yc], bx.at[b, y], loc_sem.at[b, 4]).start()

            def step(i, carry):
                other, peer = yc_peer(i)
                send(ox.at[other], bx.at[b, y], bxs.at[b], bxr.at[b], peer)
                return carry

            lax.fori_loop(1, 8, step, 0)

    def back(b):
        arrived(by.at[b, pl.ds(0, 3)], byr.at[b])
        pltpu.make_async_copy(oy.at[b, x], by.at[b, x], loc_sem.at[b, 3]).wait()

        @pl.when(core == b)
        def _():
            arrived(bx.at[b, pl.ds(0, 3)], bxr.at[b])
            pltpu.make_async_copy(ox.at[yc], bx.at[b, y], loc_sem.at[b, 4]).wait()

        @pl.when(core != b)
        def _():
            arrived(bx.at[b], bxr.at[b])

        def add(i, carry):
            high, part = i // 4, i % 4
            sm[b, i] = (bx[b, high, part].astype(F32) + by[b, part, high].astype(F32)).astype(BF)
            return carry

        lax.fori_loop(0, NZ, add, 0)
        pltpu.make_async_copy(sm.at[b, z], h.at[b, z], loc_sem.at[b, 5]).start()

        def step(i, carry):
            other, peer = z_peer(i)
            send(sm.at[b, other], h.at[b, z], rs.at[b], rr.at[b], peer)
            return carry

        lax.fori_loop(1, NZ, step, 0)

    def finish(b):
        arrived(h.at[b, pl.ds(0, NZ - 1)], rr.at[b])
        pltpu.make_async_copy(sm.at[b, z], h.at[b, z], loc_sem.at[b, 5]).wait()

        def step(i, carry):
            four = pl.ds(i * 4, 4)
            mixed = (tm[b, i].astype(F32) + h[b, four].astype(F32)).astype(BF)
            update = jnp.dot(mixed.reshape(128, D), wos[...], preferred_element_type=F32)
            res[b, four] = (t_s[b, four].astype(F32) + update.reshape(4, ROWS, D)).astype(BF)
            return carry

        lax.fori_loop(0, 4, step, 0)
        pltpu.make_async_copy(res.at[b], out.at[b], out_sem.at[b]).start()

    loads[0].wait()
    normalize(0)
    pl.semaphore_wait(barrier, 25)
    forward(0)
    loads[1].wait()
    normalize(1)
    forward(1)
    loads[2].wait()
    time_lines(0)
    time_lines(1)
    for b in range(2):
        spread(b)
        y_lines(b)
        x_lines(b)
        back(b)
    loads[3].wait()
    finish(0)
    finish(1)
    for b in range(2):
        pltpu.make_async_copy(res.at[b], out.at[b], out_sem.at[b]).wait()
        arrived(xn.at[b, pl.ds(0, NZ - 1)], zs.at[b])
        arrived(ry.at[b, pl.ds(0, 3)], ys.at[b])
        arrived(by.at[b, pl.ds(0, 3)], bys.at[b])
        arrived(h.at[b, pl.ds(0, NZ - 1)], rs.at[b])

        @pl.when(core == b)
        def _():
            arrived(r1.at[b, pl.ds(0, 3)], xs.at[b])
            arrived(ox.at[pl.ds(0, 7)], bxs.at[b])

        @pl.when(core != b)
        def _():
            arrived(r1.at[b], xs.at[b])


def body(tokens, norm_gain, w_qkv, w_out):
    shape = tokens.shape
    dma = pltpu.SemaphoreType.DMA
    result = pl.pallas_call(
        kernel,
        out_shape=jax.ShapeDtypeStruct((2, NZ, ROWS, D), BF),
        in_specs=[
            pl.BlockSpec(memory_space=pl.ANY),
            pl.BlockSpec(memory_space=pltpu.VMEM),
            pl.BlockSpec(memory_space=pl.ANY),
            pl.BlockSpec(memory_space=pl.ANY),
        ],
        out_specs=pl.BlockSpec(memory_space=pl.ANY),
        scratch_shapes=[
            pltpu.VMEM((2, NZ, ROWS, D), BF),
            pltpu.VMEM((2, NZ, ROWS, D), BF),
            pltpu.VMEM((2, 4, 4, ROWS, D), BF),
            pltpu.VMEM((2, 4, 4, ROWS, D), BF),
            pltpu.VMEM((8, 4, ROWS, D), BF),
            pltpu.VMEM((2, 4, 4, ROWS, D), BF),
            pltpu.VMEM((8, 4, ROWS, D), BF),
            pltpu.VMEM((2, 4, 4, ROWS, D), BF),
            pltpu.VMEM((2, 4, 4, ROWS, D), BF),
            pltpu.VMEM((2, NZ, ROWS, D), BF),
            pltpu.VMEM((2, NZ, ROWS, D), BF),
            pltpu.VMEM((2, 4, 4, ROWS, D), BF),
            pltpu.VMEM((2, NZ, ROWS, D), BF),
            pltpu.VMEM((12, 1024, 128), F32),
            pltpu.VMEM((4, 1024, 128), F32),
            pltpu.VMEM((D, 3 * D), BF),
            pltpu.VMEM((D, D), BF),
            dma((4,)),
            dma((2, 6)),
        ]
        + [dma((2,))] * 13,
        compiler_params=pltpu.CompilerParams(
            collective_id=0, has_side_effects=True, vmem_limit_bytes=48 * 1024 * 1024
        ),
        name="axial",
    )(tokens.reshape(2, NZ, ROWS, D), norm_gain.reshape(1, D), w_qkv, w_out)
    return result.reshape(shape)


def solution(mesh):
    placed = (P(None, None, "gx", "gy", None), P(), P(), P())
    return jax.shard_map(
        body, mesh=mesh, in_specs=placed, out_specs=P(None, None, "gx", "gy", None), check_vma=False
    )
```

```python
import jax
import jax.numpy as jnp
from jax import lax
from jax.experimental import pallas as pl
from jax.experimental.pallas import tpu as pltpu
from jax.sharding import PartitionSpec as P

NZ = 16
ROWS = 32
D = 512
MESH = pl.DeviceIdType.MESH
BF = jnp.bfloat16
F32 = jnp.float32


def device(y, zl, core, x, zh):
    return ((y * 4 + zl) * 2 + core, x * 4 + zh)


def kernel(
    tok, gain, wq, wo, out,
    t_s, xn, r1, ry, rx, oy, ox, by, bx, sm, h, tm, qkv, of, sc, wt, w, wos,
    load_sem, w_sem, loc_sem, zs, zr, ys, yr, xs, xr, bys, byr, bxs, bxr, rs, rr,
):
    gx, gy = lax.axis_index("gx"), lax.axis_index("gy")
    y, zl, core = gx // 8, (gx // 2) % 4, gx % 2
    x, zh = gy // 4, gy % 4
    z = zh * 4 + zl
    yc = y * 2 + core

    for b in range(2):
        pltpu.make_async_copy(tok.at[b], t_s.at[b], load_sem.at[b]).start()

    barrier = pltpu.get_barrier_semaphore()

    def z_peer(i):
        other = (z + (i % 2) * ((i + 1) // 2) + (1 - i % 2) * (NZ - i // 2)) % NZ
        return other, device(y, other % 4, core, x, other // 4)

    def x_peer(i):
        other = (x + i) % 4
        return other, device(y, zl, core, other, zh)

    def yc_peer(i):
        other = (yc + i) % 8
        return other, device(other // 2, zl, other % 2, x, zh)

    def each(first, last, step):
        def run(i, carry):
            step(i)
            return carry

        lax.fori_loop(first, last, run, 0)

    def greet(peer):
        return lambda i: pl.semaphore_signal(barrier, inc=1, device_id=peer(i)[1], device_id_type=MESH)

    each(1, NZ, greet(z_peer))
    each(1, 4, greet(x_peer))
    each(1, 8, greet(yc_peer))

    def weight_load(pair, kind):
        cols = pl.ds(pl.multiple_of(kind * D + pair * 128, 128), 128)
        return pltpu.make_async_copy(wq.at[:, cols], w.at[pair, kind], w_sem.at[pair, kind])

    out_load = pltpu.make_async_copy(wo, wos, load_sem.at[2])
    for pair in range(4):
        for kind in range(3):
            weight_load(pair, kind).start()
    out_load.start()

    scale = gain[...]

    def normalize(b):
        def step(i):
            two = pl.ds(i * 2, 2)
            field = t_s[b, two].astype(F32)
            mean = jnp.mean(field * field, axis=-1, keepdims=True)
            xn[b, two] = (field * lax.rsqrt(mean + 1e-05) * scale).astype(BF)

        each(0, NZ // 2, step)

    def send(src, dst, ssem, rsem, peer):
        pltpu.make_async_remote_copy(
            src_ref=src, dst_ref=dst, send_sem=ssem, recv_sem=rsem, device_id=peer, device_id_type=MESH
        ).start()

    def keep(src, dst):
        copy = pltpu.make_async_copy(src, dst, loc_sem)
        copy.start()
        copy.wait()

    def arrived(ref, sem):
        pltpu.make_async_copy(ref, ref, sem).wait()

    def forward(b):
        def step(i):
            other, peer = z_peer(i)
            send(xn.at[b, other], r1.at[b, z], zs.at[b], zr.at[b, z], peer)

        each(1, NZ, step)
        keep(xn.at[b, z], r1.at[b, z])

    def spread(b):
        def pass_on(other):
            high, low_part = other // 4, other % 4
            block = r1.at[b, other]

            @pl.when((high != y) | (core != b))
            def _():
                send(block, rx.at[yc, low_part], xs.at[b], xr.at[b], device(high, zl, b, x, zh))

            @pl.when(low_part != x)
            def _():
                send(block, ry.at[b, x, high], ys.at[b], yr.at[b], device(y, zl, core, low_part, zh))

            @pl.when((high == y) & (core == b))
            def _():
                keep(block, rx.at[yc, low_part])

            @pl.when(low_part == x)
            def _():
                keep(block, ry.at[b, x, high])

        def step(i):
            other, _ = z_peer(i)
            arrived(r1.at[b, other], zr.at[b, other])
            pass_on(other)

        pass_on(z)
        each(1, NZ, step)

    def project(src, pair, tiles):
        weights = jnp.concatenate([w[pair, kind] for kind in range(3)], axis=1)

        def step(i):
            rows = pl.ds(pl.multiple_of(i * 512, 512), 512)
            part = jnp.dot(src[pl.ds(i * 16, 16)].reshape(512, D), weights, preferred_element_type=F32)
            for kind in range(3):
                qkv[kind, rows] = part[:, 128 * kind : 128 * kind + 128]

        if tiles == 1:
            step(0)
        else:
            each(0, tiles, step)

    low = lax.broadcasted_iota(jnp.int32, (128, 128), 1) < 64
    ones = jnp.ones((128, 128), BF)

    def lines(units, mask):
        def first(slot, load, store):
            q = load(0) * 0.125
            k = load(1).astype(BF)
            both = jnp.concatenate([jnp.where(low, q, 0.0), jnp.where(low, 0.0, q)], axis=0).astype(BF)
            scores = lax.dot_general(both, k, (((1,), (1,)), ((), ())), preferred_element_type=F32)
            if mask is not None:
                scores = jnp.where(mask, scores, -3e38)
            sc[slot] = scores

        def second(slot, load, store):
            scores = sc[slot]
            wt[slot] = jnp.exp(scores - jnp.max(scores, axis=-1, keepdims=True)).astype(BF)

        def third(slot, load, store):
            v = load(2).astype(BF)
            total = jnp.dot(wt[slot], jnp.concatenate([v, ones], axis=1), preferred_element_type=F32)
            part = jnp.where(low, total[:128, :128], total[128:, :128])
            norm = jnp.where(low, total[:128, 128:], total[128:, 128:])
            store(part / norm)

        for u in range(len(units) + 2):
            if u < len(units):
                first(u, *units[u])
            if 1 <= u <= len(units):
                second(u - 1, *units[u - 1])
            if u >= 2:
                third(u - 2, *units[u - 2])

    def aligned(c):
        def rows(g):
            return pl.ds(g * ROWS + c * 8, 8)

        def load(kind):
            return jnp.concatenate([qkv[kind, rows(g)] for g in range(16)], axis=0)

        def store(value):
            for g in range(16):
                of[rows(g)] = value[8 * g : 8 * g + 8]

        return load, store

    def strided(c):
        def load(kind):
            return qkv[kind, pl.ds(c, 128, stride=8)]

        def store(value):
            of[pl.ds(c, 128, stride=8)] = value

        return load, store

    def rounded(dst, blocks):
        def step(i):
            rows = pl.ds(pl.multiple_of(i * 256, 256), 256)
            dst[pl.ds(i * 8, 8)] = of[rows].reshape(8, ROWS, 128).astype(BF)

        each(0, blocks // 8, step)

    row = lax.broadcasted_iota(jnp.int32, (256, 128), 0)
    column = lax.broadcasted_iota(jnp.int32, (256, 128), 1)
    same_cell = (row % 8) == (column % 8)

    def time_lines(b):
        def step(pair):
            project(xn.at[b], pair, 1)
            lines([aligned(c) for c in range(4)], same_cell)
            rounded(tm.at[b, pair], 16)

        each(0, 4, step)

    def attend(b):
        arrived(ry.at[b, pl.ds(0, 3)], yr.at[b])

        @pl.when(core == b)
        def _():
            arrived(rx.at[pl.ds(0, 7)], xr.at[b])

        def step(pair):
            @pl.when(core == b)
            def _():
                project(rx_rows, pair, 2)
                lines([strided(c) for c in range(8)], None)
                rounded(ox.at[pair], 32)

                def give(i):
                    other, peer = yc_peer(i)
                    send(ox.at[pair, pl.ds(other * 4, 4)], bx.at[b, pair, y], bxs.at[pair], bxr.at[b, pair], peer)

                each(1, 8, give)
                keep(ox.at[pair, pl.ds(yc * 4, 4)], bx.at[b, pair, y])

            project(ry_rows.at[b], pair, 1)
            lines([aligned(c) for c in range(4)], None)
            rounded(oy.at[b, pair], 16)

            def give(i):
                other, peer = x_peer(i)
                send(oy.at[b, pair, pl.ds(other * 4, 4)], by.at[b, pair, x], bys.at[b, pair], byr.at[b, pair], peer)

            each(1, 4, give)
            keep(oy.at[b, pair, pl.ds(x * 4, 4)], by.at[b, pair, x])

        each(0, 4, step)

    rx_rows = rx.reshape(32, ROWS, D)
    ry_rows = ry.reshape(2, 16, ROWS, D)

    def back(b):
        def step(pair):
            arrived(by.at[b, pair, pl.ds(0, 3)], byr.at[b, pair])

            @pl.when(core == b)
            def _():
                arrived(bx.at[b, pair, pl.ds(0, 3)], bxr.at[b, pair])

            @pl.when(core != b)
            def _():
                arrived(bx.at[b, pair], bxr.at[b, pair])

            for high in range(4):
                for part in range(4):
                    total = bx[b, pair, high, part].astype(F32) + by[b, pair, part, high].astype(F32)
                    sm[b, pair, 4 * high + part] = total.astype(BF)

            def give(i):
                other, peer = z_peer(i)
                send(sm.at[b, pair, other], h.at[b, pair, z], rs.at[b, pair], rr.at[b, pair], peer)

            each(1, NZ, give)
            keep(sm.at[b, pair, z], h.at[b, pair, z])

        each(0, 4, step)

    def finish(b):
        each(0, 4, lambda pair: arrived(h.at[b, pair, pl.ds(0, NZ - 1)], rr.at[b, pair]))

        def step(i):
            four = pl.ds(i * 4, 4)
            mixed = jnp.concatenate(
                [
                    (tm[b, pair, four].astype(F32) + h[b, pair, four].astype(F32)).reshape(128, 128)
                    for pair in range(4)
                ],
                axis=1,
            ).astype(BF)
            update = jnp.dot(mixed, wos[...], preferred_element_type=F32)
            out[b, four] = (t_s[b, four].astype(F32) + update.reshape(4, ROWS, D)).astype(BF)

        each(0, 4, step)

    pltpu.make_async_copy(tok.at[0], t_s.at[0], load_sem.at[0]).wait()
    normalize(0)
    pl.semaphore_wait(barrier, 25)
    forward(0)
    pltpu.make_async_copy(tok.at[1], t_s.at[1], load_sem.at[1]).wait()
    normalize(1)
    forward(1)
    for pair in range(4):
        for kind in range(3):
            weight_load(pair, kind).wait()
    time_lines(0)
    time_lines(1)
    for b in range(2):
        spread(b)
        attend(b)
        back(b)
    out_load.wait()
    finish(0)
    finish(1)
    for b in range(2):
        arrived(xn.at[b, pl.ds(0, NZ - 1)], zs.at[b])
        arrived(ry.at[b, pl.ds(0, 3)], ys.at[b])

        @pl.when(core == b)
        def _():
            arrived(r1.at[b, pl.ds(0, 12)], xs.at[b])
            each(0, 4, lambda pair: arrived(ox.at[pair, pl.ds(0, 28)], bxs.at[pair]))

        @pl.when(core != b)
        def _():
            arrived(r1.at[b], xs.at[b])

        def drain(pair):
            arrived(by.at[b, pair, pl.ds(0, 3)], bys.at[b, pair])
            arrived(h.at[b, pair, pl.ds(0, NZ - 1)], rs.at[b, pair])

        each(0, 4, drain)


def body(tokens, norm_gain, w_qkv, w_out):
    shape = tokens.shape
    dma = pltpu.SemaphoreType.DMA
    result = pl.pallas_call(
        kernel,
        out_shape=jax.ShapeDtypeStruct((2, NZ, ROWS, D), BF),
        in_specs=[
            pl.BlockSpec(memory_space=pltpu.HBM),
            pl.BlockSpec(memory_space=pltpu.VMEM),
            pl.BlockSpec(memory_space=pltpu.HBM),
            pl.BlockSpec(memory_space=pltpu.HBM),
        ],
        out_specs=pl.BlockSpec(memory_space=pltpu.VMEM),
        scratch_shapes=[
            pltpu.VMEM((2, NZ, ROWS, D), BF),
            pltpu.VMEM((2, NZ, ROWS, D), BF),
            pltpu.VMEM((2, NZ, ROWS, D), BF),
            pltpu.VMEM((2, 4, 4, ROWS, D), BF),
            pltpu.VMEM((8, 4, ROWS, D), BF),
            pltpu.VMEM((2, 4, NZ, ROWS, 128), BF),
            pltpu.VMEM((4, 32, ROWS, 128), BF),
            pltpu.VMEM((2, 4, 4, 4, ROWS, 128), BF),
            pltpu.VMEM((2, 4, 4, 4, ROWS, 128), BF),
            pltpu.VMEM((2, 4, NZ, ROWS, 128), BF),
            pltpu.VMEM((2, 4, NZ, ROWS, 128), BF),
            pltpu.VMEM((2, 4, NZ, ROWS, 128), BF),
            pltpu.VMEM((3, 1024, 128), F32),
            pltpu.VMEM((1024, 128), F32),
            pltpu.VMEM((8, 256, 128), F32),
            pltpu.VMEM((8, 256, 128), BF),
            pltpu.VMEM((4, 3, D, 128), BF),
            pltpu.VMEM((D, D), BF),
            dma((3,)),
            dma((4, 3)),
            dma,
            dma((2,)),
            dma((2, NZ)),
        ]
        + [dma((2,))] * 4
        + [dma((2, 4)), dma((2, 4)), dma((4,)), dma((2, 4)), dma((2, 4)), dma((2, 4))],
        compiler_params=pltpu.CompilerParams(
            collective_id=0, has_side_effects=True, vmem_limit_bytes=48 * 1024 * 1024
        ),
        name="axial",
    )(tokens.reshape(2, NZ, ROWS, D), norm_gain.reshape(1, D), w_qkv, w_out)
    return result.reshape(shape)


def solution(mesh):
    placed = (P(None, None, "gx", "gy", None), P(), P(), P())
    return jax.shard_map(
        body, mesh=mesh, in_specs=placed, out_specs=P(None, None, "gx", "gy", None), check_vma=False
    )
```

```python
import jax
import jax.numpy as jnp
from jax import lax
from jax.experimental import pallas as pl
from jax.experimental.pallas import tpu as pltpu
from jax.sharding import PartitionSpec as P

NZ = 16
ROWS = 32
D = 512
MESH = pl.DeviceIdType.MESH
BF = jnp.bfloat16
F32 = jnp.float32


def device(y, zl, core, x, zh):
    return ((y * 4 + zl) * 2 + core, x * 4 + zh)


def kernel(
    tok, gain, wq, wo, out,
    t_s, xn, r1, ry, rx, oy, ox, by, bx, sm, h, tm, res, qkv, of, sc, wt, w, wos, gains,
    load_sem, w_sem, loc_sem, out_sem, near_sem, zs, zr, ys, yr, xs, xr, bys, byr, bxs, bxr, rs, rr,
):
    gx, gy = lax.axis_index("gx"), lax.axis_index("gy")
    y, zl, core = gx // 8, (gx // 2) % 4, gx % 2
    x, zh = gy // 4, gy % 4
    z = zh * 4 + zl
    yc = y * 2 + core

    gain_load = pltpu.make_async_copy(gain, gains, load_sem.at[3])
    gain_load.start()
    for b in range(2):
        pltpu.make_async_copy(tok.at[b], t_s.at[b], load_sem.at[b]).start()

    barrier = pltpu.get_barrier_semaphore()

    def z_peer(i):
        other = (z + (i % 2) * ((i + 1) // 2) + (1 - i % 2) * (NZ - i // 2)) % NZ
        return other, device(y, other % 4, core, x, other // 4)

    def x_peer(i):
        other = (x + i) % 4
        return other, device(y, zl, core, other, zh)

    def yc_peer(i):
        other = (yc + i) % 8
        return other, device(other // 2, zl, other % 2, x, zh)

    def each(first, last, step):
        def run(i, carry):
            step(i)
            return carry

        lax.fori_loop(first, last, run, 0)

    def greet(peer):
        return lambda i: pl.semaphore_signal(barrier, inc=1, device_id=peer(i)[1], device_id_type=MESH)

    each(1, 3, greet(z_peer))
    each(1, 4, greet(x_peer))
    each(1, 8, greet(yc_peer))

    def weight_load(pair, kind):
        cols = pl.ds(pl.multiple_of(kind * D + pair * 128, 128), 128)
        return pltpu.make_async_copy(wq.at[:, cols], w.at[pair, kind], w_sem.at[pair, kind])

    out_load = pltpu.make_async_copy(wo, wos, load_sem.at[2])
    for pair in range(4):
        for kind in range(3):
            weight_load(pair, kind).start()
    out_load.start()

    def normalize(b):
        def step(i):
            two = pl.ds(i * 2, 2)
            field = t_s[b, two].astype(F32)
            mean = jnp.mean(field * field, axis=-1, keepdims=True)
            xn[b, two] = (field * lax.rsqrt(mean + 1e-05) * gains[...]).astype(BF)

        each(0, NZ // 2, step)

    def send(src, dst, ssem, rsem, peer):
        pltpu.make_async_remote_copy(
            src_ref=src, dst_ref=dst, send_sem=ssem, recv_sem=rsem, device_id=peer, device_id_type=MESH
        ).start()

    def keep(src, dst):
        copy = pltpu.make_async_copy(src, dst, loc_sem)
        copy.start()
        copy.wait()

    def arrived(ref, sem):
        pltpu.make_async_copy(ref, ref, sem).wait()

    def forward_to(b, i):
        other, peer = z_peer(i)
        send(xn.at[b, other], r1.at[b, z], zs.at[b], zr.at[b, z], peer)

    def tell(level):
        for side in range(2):
            pl.semaphore_signal(near_sem.at[side, level], inc=1, device_id=z_peer(side + 1)[1], device_id_type=MESH)

    def forward_first():
        def step(level):
            tell(level)
            forward_to(0, 2 * level - 1)
            forward_to(0, 2 * level)
            for side in range(2):
                pl.semaphore_wait(near_sem.at[side, level], 1)

        each(1, 8, step)
        forward_to(0, 15)
        keep(xn.at[0, z], r1.at[0, z])

    def forward_second():
        each(1, NZ, lambda i: forward_to(1, i))
        keep(xn.at[1, z], r1.at[1, z])

    def spread(b):
        def pass_on(other):
            high, low_part = other // 4, other % 4
            block = r1.at[b, other]

            @pl.when((high != y) | (core != b))
            def _():
                send(block, rx.at[yc, low_part], xs.at[b], xr.at[b], device(high, zl, b, x, zh))

            @pl.when(low_part != x)
            def _():
                send(block, ry.at[b, x, high], ys.at[b], yr.at[b], device(y, zl, core, low_part, zh))

            @pl.when((high == y) & (core == b))
            def _():
                keep(block, rx.at[yc, low_part])

            @pl.when(low_part == x)
            def _():
                keep(block, ry.at[b, x, high])

        def step(i):
            other, _ = z_peer(i)
            arrived(r1.at[b, other], zr.at[b, other])
            pass_on(other)

        pass_on(z)
        each(1, NZ, step)

    def project(src, pair, tiles):
        weights = jnp.concatenate([w[pair, kind] for kind in range(3)], axis=1)

        def step(i):
            rows = pl.ds(pl.multiple_of(i * 512, 512), 512)
            part = jnp.dot(src[pl.ds(i * 16, 16)].reshape(512, D), weights, preferred_element_type=F32)
            for kind in range(3):
                qkv[kind, rows] = part[:, 128 * kind : 128 * kind + 128]

        if tiles == 1:
            step(0)
        else:
            each(0, tiles, step)

    low = lax.broadcasted_iota(jnp.int32, (128, 128), 1) < 64
    ones = jnp.ones((128, 128), BF)

    def lines(units, mask):
        def first(slot, load, store):
            q = load(0) * 0.125
            k = load(1).astype(BF)
            both = jnp.concatenate([jnp.where(low, q, 0.0), jnp.where(low, 0.0, q)], axis=0).astype(BF)
            scores = lax.dot_general(both, k, (((1,), (1,)), ((), ())), preferred_element_type=F32)
            if mask is not None:
                scores = jnp.where(mask, scores, -3e38)
            sc[slot] = scores

        def second(slot, load, store):
            scores = sc[slot]
            wt[slot] = jnp.exp(scores - jnp.max(scores, axis=-1, keepdims=True)).astype(BF)

        def third(slot, load, store):
            v = load(2).astype(BF)
            total = jnp.dot(wt[slot], jnp.concatenate([v, ones], axis=1), preferred_element_type=F32)
            part = jnp.where(low, total[:128, :128], total[128:, :128])
            norm = jnp.where(low, total[:128, 128:], total[128:, 128:])
            store(part / norm)

        for u in range(len(units) + 2):
            if u < len(units):
                first(u, *units[u])
            if 1 <= u <= len(units):
                second(u - 1, *units[u - 1])
            if u >= 2:
                third(u - 2, *units[u - 2])

    def aligned(c):
        def rows(g):
            return pl.ds(g * ROWS + c * 8, 8)

        def load(kind):
            return jnp.concatenate([qkv[kind, rows(g)] for g in range(16)], axis=0)

        def store(value):
            for g in range(16):
                of[rows(g)] = value[8 * g : 8 * g + 8]

        return load, store

    def strided(c):
        def load(kind):
            return qkv[kind, pl.ds(c, 128, stride=8)]

        def store(value):
            of[pl.ds(c, 128, stride=8)] = value

        return load, store

    def rounded(dst, blocks):
        def step(i):
            rows = pl.ds(pl.multiple_of(i * 256, 256), 256)
            dst[pl.ds(i * 8, 8)] = of[rows].reshape(8, ROWS, 128).astype(BF)

        each(0, blocks // 8, step)

    row = lax.broadcasted_iota(jnp.int32, (256, 128), 0)
    column = lax.broadcasted_iota(jnp.int32, (256, 128), 1)
    same_cell = (row % 8) == (column % 8)

    def time_lines(b):
        def step(pair):
            project(xn.at[b], pair, 1)
            lines([aligned(c) for c in range(4)], same_cell)
            rounded(tm.at[b, pair], 16)

        each(0, 4, step)

    def attend(b):
        arrived(ry.at[b, pl.ds(0, 3)], yr.at[b])

        @pl.when(core == b)
        def _():
            arrived(rx.at[pl.ds(0, 7)], xr.at[b])

        def step(pair):
            @pl.when(core == b)
            def _():
                project(rx_rows, pair, 2)
                lines([strided(c) for c in range(8)], None)
                rounded(ox.at[pair], 32)

                def give(i):
                    other, peer = yc_peer(i)
                    send(ox.at[pair, pl.ds(other * 4, 4)], bx.at[b, pair, y], bxs.at[pair], bxr.at[b, pair], peer)

                each(1, 8, give)
                keep(ox.at[pair, pl.ds(yc * 4, 4)], bx.at[b, pair, y])

            project(ry_rows.at[b], pair, 1)
            lines([aligned(c) for c in range(4)], None)
            rounded(oy.at[b, pair], 16)

            def give(i):
                other, peer = x_peer(i)
                send(oy.at[b, pair, pl.ds(other * 4, 4)], by.at[b, pair, x], bys.at[b, pair], byr.at[b, pair], peer)

            each(1, 4, give)
            keep(oy.at[b, pair, pl.ds(x * 4, 4)], by.at[b, pair, x])

            @pl.when(pair >= 1)
            def _():
                back(b, pair - 1)

        each(0, 4, step)
        back(b, 3)

    rx_rows = rx.reshape(32, ROWS, D)
    ry_rows = ry.reshape(2, 16, ROWS, D)

    def back(b, pair):
        arrived(by.at[b, pair, pl.ds(0, 3)], byr.at[b, pair])

        @pl.when(core == b)
        def _():
            arrived(bx.at[b, pair, pl.ds(0, 3)], bxr.at[b, pair])

        @pl.when(core != b)
        def _():
            arrived(bx.at[b, pair], bxr.at[b, pair])

        for high in range(4):
            for part in range(4):
                total = bx[b, pair, high, part].astype(F32) + by[b, pair, part, high].astype(F32)
                sm[b, pair, 4 * high + part] = total.astype(BF)

        def give(i):
            other, peer = z_peer(NZ - i)
            send(sm.at[b, pair, other], h.at[b, pair, z], rs.at[b, pair], rr.at[b, pair], peer)

        each(1, NZ, give)
        keep(sm.at[b, pair, z], h.at[b, pair, z])


    def finish(b):
        each(0, 4, lambda pair: arrived(h.at[b, pair, pl.ds(0, NZ - 1)], rr.at[b, pair]))

        def step(i):
            four = pl.ds(i * 4, 4)
            mixed = jnp.concatenate(
                [
                    (tm[b, pair, four].astype(F32) + h[b, pair, four].astype(F32)).reshape(128, 128)
                    for pair in range(4)
                ],
                axis=1,
            ).astype(BF)
            update = jnp.dot(mixed, wos[...], preferred_element_type=F32)
            res[b, four] = (t_s[b, four].astype(F32) + update.reshape(4, ROWS, D)).astype(BF)
            pltpu.make_async_copy(res.at[b, four], out.at[b, four], out_sem.at[b]).start()

        each(0, 4, step)

    pltpu.make_async_copy(tok.at[0], t_s.at[0], load_sem.at[0]).wait()
    gain_load.wait()
    normalize(0)
    pl.semaphore_wait(barrier, 12)
    forward_first()
    pltpu.make_async_copy(tok.at[1], t_s.at[1], load_sem.at[1]).wait()
    normalize(1)
    forward_second()
    for pair in range(4):
        for kind in range(3):
            weight_load(pair, kind).wait()
    time_lines(0)
    time_lines(1)
    for b in range(2):
        spread(b)
        attend(b)
    out_load.wait()
    finish(0)
    finish(1)
    for b in range(2):
        arrived(xn.at[b, pl.ds(0, NZ - 1)], zs.at[b])
        arrived(ry.at[b, pl.ds(0, 3)], ys.at[b])

        @pl.when(core == b)
        def _():
            arrived(r1.at[b, pl.ds(0, 12)], xs.at[b])
            each(0, 4, lambda pair: arrived(ox.at[pair, pl.ds(0, 28)], bxs.at[pair]))

        @pl.when(core != b)
        def _():
            arrived(r1.at[b], xs.at[b])

        def drain(pair):
            arrived(by.at[b, pair, pl.ds(0, 3)], bys.at[b, pair])
            arrived(h.at[b, pair, pl.ds(0, NZ - 1)], rs.at[b, pair])

        each(0, 4, drain)
        pltpu.make_async_copy(res.at[b], out.at[b], out_sem.at[b]).wait()


def body(tokens, norm_gain, w_qkv, w_out):
    shape = tokens.shape
    dma = pltpu.SemaphoreType.DMA
    result = pl.pallas_call(
        kernel,
        out_shape=jax.ShapeDtypeStruct((2, NZ, ROWS, D), BF),
        in_specs=[
            pl.BlockSpec(memory_space=pl.ANY),
            pl.BlockSpec(memory_space=pl.ANY),
            pl.BlockSpec(memory_space=pl.ANY),
            pl.BlockSpec(memory_space=pl.ANY),
        ],
        out_specs=pl.BlockSpec(memory_space=pl.ANY),
        scratch_shapes=[
            pltpu.VMEM((2, NZ, ROWS, D), BF),
            pltpu.VMEM((2, NZ, ROWS, D), BF),
            pltpu.VMEM((2, NZ, ROWS, D), BF),
            pltpu.VMEM((2, 4, 4, ROWS, D), BF),
            pltpu.VMEM((8, 4, ROWS, D), BF),
            pltpu.VMEM((2, 4, NZ, ROWS, 128), BF),
            pltpu.VMEM((4, 32, ROWS, 128), BF),
            pltpu.VMEM((2, 4, 4, 4, ROWS, 128), BF),
            pltpu.VMEM((2, 4, 4, 4, ROWS, 128), BF),
            pltpu.VMEM((2, 4, NZ, ROWS, 128), BF),
            pltpu.VMEM((2, 4, NZ, ROWS, 128), BF),
            pltpu.VMEM((2, 4, NZ, ROWS, 128), BF),
            pltpu.VMEM((2, NZ, ROWS, D), BF),
            pltpu.VMEM((3, 1024, 128), F32),
            pltpu.VMEM((1024, 128), F32),
            pltpu.VMEM((8, 256, 128), F32),
            pltpu.VMEM((8, 256, 128), BF),
            pltpu.VMEM((4, 3, D, 128), BF),
            pltpu.VMEM((D, D), BF),
            pltpu.VMEM((1, D), F32),
            dma((4,)),
            dma((4, 3)),
            dma,
            dma((2,)),
            pltpu.SemaphoreType.REGULAR((2, 8)),
            dma((2,)),
            dma((2, NZ)),
        ]
        + [dma((2,))] * 4
        + [dma((2, 4)), dma((2, 4)), dma((4,)), dma((2, 4)), dma((2, 4)), dma((2, 4))],
        compiler_params=pltpu.CompilerParams(
            collective_id=0, has_side_effects=True, vmem_limit_bytes=67043328
        ),
        name="axial",
    )(tokens.reshape(2, NZ, ROWS, D), norm_gain.reshape(1, D), w_qkv, w_out)
    return result.reshape(shape)


def solution(mesh):
    placed = (P(None, None, "gx", "gy", None), P(), P(), P())
    return jax.shard_map(
        body, mesh=mesh, in_specs=placed, out_specs=P(None, None, "gx", "gy", None), check_vma=False
    )
```

```python
import jax
import jax.numpy as jnp
from jax import lax
from jax.experimental import pallas as pl
from jax.experimental.pallas import tpu as pltpu
from jax.sharding import PartitionSpec as P

NZ = 16
ROWS = 32
D = 512
MESH = pl.DeviceIdType.MESH
BF = jnp.bfloat16
F32 = jnp.float32


def device(y, zl, core, x, zh):
    return ((y * 4 + zl) * 2 + core, x * 4 + zh)


def kernel(
    tok, gain, wq, wo, out,
    t_s, xn, r1, ry, rx, oy, ox, by, bx, sm, h, tm, qkv, of, sc, wt, w, wos, gains,
    load_sem, w_sem, loc_sem, near_sem, zs, zr, ys, yr, xs, xr, bys, byr, bxs, bxr, rs, rr,
):
    gx, gy = lax.axis_index("gx"), lax.axis_index("gy")
    y, zl, core = gx // 8, (gx // 2) % 4, gx % 2
    x, zh = gy // 4, gy % 4
    z = zh * 4 + zl
    yc = y * 2 + core

    gain_load = pltpu.make_async_copy(gain, gains, load_sem.at[3])
    gain_load.start()
    for b in range(2):
        pltpu.make_async_copy(tok.at[b], t_s.at[b], load_sem.at[b]).start()

    barrier = pltpu.get_barrier_semaphore()

    def z_peer(i):
        other = (z + (i % 2) * ((i + 1) // 2) + (1 - i % 2) * (NZ - i // 2)) % NZ
        return other, device(y, other % 4, core, x, other // 4)

    def x_peer(i):
        other = (x + i) % 4
        return other, device(y, zl, core, other, zh)

    def yc_peer(i):
        other = (yc + i) % 8
        return other, device(other // 2, zl, other % 2, x, zh)

    def each(first, last, step):
        def run(i, carry):
            step(i)
            return carry

        lax.fori_loop(first, last, run, 0)

    def greet(peer):
        return lambda i: pl.semaphore_signal(barrier, inc=1, device_id=peer(i)[1], device_id_type=MESH)

    each(1, 3, greet(z_peer))
    each(1, 4, greet(x_peer))
    each(1, 8, greet(yc_peer))

    def weight_load(pair, kind):
        cols = pl.ds(pl.multiple_of(kind * D + pair * 128, 128), 128)
        return pltpu.make_async_copy(wq.at[:, cols], w.at[pair, kind], w_sem.at[pair, kind])

    out_load = pltpu.make_async_copy(wo, wos, load_sem.at[2])
    for pair in range(4):
        for kind in range(3):
            weight_load(pair, kind).start()
    out_load.start()

    def normalize(b):
        def step(i):
            two = pl.ds(i * 2, 2)
            field = t_s[b, two].astype(F32)
            mean = jnp.mean(field * field, axis=-1, keepdims=True)
            xn[b, two] = (field * lax.rsqrt(mean + 1e-05) * gains[...]).astype(BF)

        each(0, NZ // 2, step)

    def send(src, dst, ssem, rsem, peer):
        pltpu.make_async_remote_copy(
            src_ref=src, dst_ref=dst, send_sem=ssem, recv_sem=rsem, device_id=peer, device_id_type=MESH
        ).start()

    def keep(src, dst):
        copy = pltpu.make_async_copy(src, dst, loc_sem)
        copy.start()
        copy.wait()

    def arrived(ref, sem):
        pltpu.make_async_copy(ref, ref, sem).wait()

    def forward_to(b, i):
        other, peer = z_peer(i)
        send(xn.at[b, other], r1.at[b, z], zs.at[b], zr.at[b, z], peer)

    def tell(level):
        for side in range(2):
            pl.semaphore_signal(near_sem.at[side, level], inc=1, device_id=z_peer(side + 1)[1], device_id_type=MESH)

    def forward_first():
        def step(level):
            tell(level)
            forward_to(0, 2 * level - 1)
            forward_to(0, 2 * level)
            for side in range(2):
                pl.semaphore_wait(near_sem.at[side, level], 1)

        each(1, 8, step)
        forward_to(0, 15)
        keep(xn.at[0, z], r1.at[0, z])

    def forward_second():
        each(1, NZ, lambda i: forward_to(1, i))
        keep(xn.at[1, z], r1.at[1, z])

    def spread(b):
        def pass_on(other):
            high, low_part = other // 4, other % 4
            block = r1.at[b, other]

            @pl.when((high != y) | (core != b))
            def _():
                send(block, rx.at[yc, low_part], xs.at[b], xr.at[b], device(high, zl, b, x, zh))

            @pl.when(low_part != x)
            def _():
                send(block, ry.at[b, x, high], ys.at[b], yr.at[b], device(y, zl, core, low_part, zh))

            @pl.when((high == y) & (core == b))
            def _():
                keep(block, rx.at[yc, low_part])

            @pl.when(low_part == x)
            def _():
                keep(block, ry.at[b, x, high])

        def step(i):
            other, _ = z_peer(i)
            arrived(r1.at[b, other], zr.at[b, other])
            pass_on(other)

        pass_on(z)
        each(1, NZ, step)

    def project(src, pair, tiles):
        weights = jnp.concatenate([w[pair, kind] for kind in range(3)], axis=1)

        def step(i):
            rows = pl.ds(pl.multiple_of(i * 512, 512), 512)
            part = jnp.dot(src[pl.ds(i * 16, 16)].reshape(512, D), weights, preferred_element_type=F32)
            for kind in range(3):
                qkv[kind, rows] = part[:, 128 * kind : 128 * kind + 128]

        if tiles == 1:
            step(0)
        else:
            each(0, tiles, step)

    low = lax.broadcasted_iota(jnp.int32, (128, 128), 1) < 64
    ones = jnp.ones((128, 128), BF)

    def lines(units, mask):
        def first(slot, load, store):
            q = load(0) * 0.125
            k = load(1).astype(BF)
            both = jnp.concatenate([jnp.where(low, q, 0.0), jnp.where(low, 0.0, q)], axis=0).astype(BF)
            scores = lax.dot_general(both, k, (((1,), (1,)), ((), ())), preferred_element_type=F32)
            if mask is not None:
                scores = jnp.where(mask, scores, -3e38)
            sc[slot] = scores

        def second(slot, load, store):
            scores = sc[slot]
            wt[slot] = jnp.exp(scores - jnp.max(scores, axis=-1, keepdims=True)).astype(BF)

        def third(slot, load, store):
            v = load(2).astype(BF)
            total = jnp.dot(wt[slot], jnp.concatenate([v, ones], axis=1), preferred_element_type=F32)
            part = jnp.where(low, total[:128, :128], total[128:, :128])
            norm = jnp.where(low, total[:128, 128:], total[128:, 128:])
            store(part / norm)

        for u in range(len(units) + 2):
            if u < len(units):
                first(u, *units[u])
            if 1 <= u <= len(units):
                second(u - 1, *units[u - 1])
            if u >= 2:
                third(u - 2, *units[u - 2])

    def aligned(c):
        def rows(g):
            return pl.ds(g * ROWS + c * 8, 8)

        def load(kind):
            return jnp.concatenate([qkv[kind, rows(g)] for g in range(16)], axis=0)

        def store(value):
            for g in range(16):
                of[rows(g)] = value[8 * g : 8 * g + 8]

        return load, store

    def strided(c):
        def load(kind):
            return qkv[kind, pl.ds(c, 128, stride=8)]

        def store(value):
            of[pl.ds(c, 128, stride=8)] = value

        return load, store

    def rounded(dst, blocks):
        def step(i):
            rows = pl.ds(pl.multiple_of(i * 256, 256), 256)
            dst[pl.ds(i * 8, 8)] = of[rows].reshape(8, ROWS, 128).astype(BF)

        each(0, blocks // 8, step)

    row = lax.broadcasted_iota(jnp.int32, (256, 128), 0)
    column = lax.broadcasted_iota(jnp.int32, (256, 128), 1)
    same_cell = (row % 8) == (column % 8)

    def time_lines(b):
        def step(pair):
            project(xn.at[b], pair, 1)
            lines([aligned(c) for c in range(4)], same_cell)
            rounded(tm.at[b, pair], 16)

        each(0, 4, step)

    def attend(b):
        arrived(ry.at[b, pl.ds(0, 3)], yr.at[b])

        @pl.when(core == b)
        def _():
            arrived(rx.at[pl.ds(0, 7)], xr.at[b])

        def step(pair):
            @pl.when(core == b)
            def _():
                project(rx_rows, pair, 2)
                lines([strided(c) for c in range(8)], None)
                rounded(ox.at[pair], 32)

                def give(i):
                    other, peer = yc_peer(i)
                    send(ox.at[pair, pl.ds(other * 4, 4)], bx.at[b, pair, y], bxs.at[pair], bxr.at[b, pair], peer)

                each(1, 8, give)
                keep(ox.at[pair, pl.ds(yc * 4, 4)], bx.at[b, pair, y])

            project(ry_rows.at[b], pair, 1)
            lines([aligned(c) for c in range(4)], None)
            rounded(oy.at[b, pair], 16)

            def give(i):
                other, peer = x_peer(i)
                send(oy.at[b, pair, pl.ds(other * 4, 4)], by.at[b, pair, x], bys.at[b, pair], byr.at[b, pair], peer)

            each(1, 4, give)
            keep(oy.at[b, pair, pl.ds(x * 4, 4)], by.at[b, pair, x])

            @pl.when(pair >= 1)
            def _():
                back(b, pair - 1)

        each(0, 4, step)
        back(b, 3)

    rx_rows = rx.reshape(32, ROWS, D)
    ry_rows = ry.reshape(2, 16, ROWS, D)

    def back(b, pair):
        arrived(by.at[b, pair, pl.ds(0, 3)], byr.at[b, pair])

        @pl.when(core == b)
        def _():
            arrived(bx.at[b, pair, pl.ds(0, 3)], bxr.at[b, pair])

        @pl.when(core != b)
        def _():
            arrived(bx.at[b, pair], bxr.at[b, pair])

        for high in range(4):
            for part in range(4):
                total = bx[b, pair, high, part].astype(F32) + by[b, pair, part, high].astype(F32)
                sm[b, pair, 4 * high + part] = total.astype(BF)

        def give(i):
            other, peer = z_peer(NZ - i)
            send(sm.at[b, pair, other], h.at[b, pair, z], rs.at[b, pair], rr.at[b, pair], peer)

        each(1, NZ, give)
        keep(sm.at[b, pair, z], h.at[b, pair, z])


    def finish(b):
        each(0, 4, lambda pair: arrived(h.at[b, pair, pl.ds(0, NZ - 1)], rr.at[b, pair]))

        def step(i):
            four = pl.ds(i * 4, 4)
            mixed = jnp.concatenate(
                [
                    (tm[b, pair, four].astype(F32) + h[b, pair, four].astype(F32)).reshape(128, 128)
                    for pair in range(4)
                ],
                axis=1,
            ).astype(BF)
            update = jnp.dot(mixed, wos[...], preferred_element_type=F32)
            out[b, four] = (t_s[b, four].astype(F32) + update.reshape(4, ROWS, D)).astype(BF)

        each(0, 4, step)

    pltpu.make_async_copy(tok.at[0], t_s.at[0], load_sem.at[0]).wait()
    gain_load.wait()
    normalize(0)
    pl.semaphore_wait(barrier, 12)
    forward_first()
    pltpu.make_async_copy(tok.at[1], t_s.at[1], load_sem.at[1]).wait()
    normalize(1)
    forward_second()
    for pair in range(4):
        for kind in range(3):
            weight_load(pair, kind).wait()
    time_lines(0)
    time_lines(1)
    for b in range(2):
        spread(b)
        attend(b)
    out_load.wait()
    finish(0)
    finish(1)
    for b in range(2):
        arrived(xn.at[b, pl.ds(0, NZ - 1)], zs.at[b])
        arrived(ry.at[b, pl.ds(0, 3)], ys.at[b])

        @pl.when(core == b)
        def _():
            arrived(r1.at[b, pl.ds(0, 12)], xs.at[b])
            each(0, 4, lambda pair: arrived(ox.at[pair, pl.ds(0, 28)], bxs.at[pair]))

        @pl.when(core != b)
        def _():
            arrived(r1.at[b], xs.at[b])

        def drain(pair):
            arrived(by.at[b, pair, pl.ds(0, 3)], bys.at[b, pair])
            arrived(h.at[b, pair, pl.ds(0, NZ - 1)], rs.at[b, pair])

        each(0, 4, drain)


def body(tokens, norm_gain, w_qkv, w_out):
    shape = tokens.shape
    dma = pltpu.SemaphoreType.DMA
    operands = (tokens.reshape(2, NZ, ROWS, D), norm_gain.reshape(1, D), w_qkv, w_out)
    result = pl.pallas_call(
        kernel,
        out_shape=jax.ShapeDtypeStruct((2, NZ, ROWS, D), BF),
        in_specs=[
            pl.BlockSpec(memory_space=pl.ANY),
            pl.BlockSpec(memory_space=pl.ANY),
            pl.BlockSpec(memory_space=pl.ANY),
            pl.BlockSpec(memory_space=pl.ANY),
        ],
        out_specs=pl.BlockSpec(memory_space=pltpu.VMEM),
        scratch_shapes=[
            pltpu.VMEM((2, NZ, ROWS, D), BF),
            pltpu.VMEM((2, NZ, ROWS, D), BF),
            pltpu.VMEM((2, NZ, ROWS, D), BF),
            pltpu.VMEM((2, 4, 4, ROWS, D), BF),
            pltpu.VMEM((8, 4, ROWS, D), BF),
            pltpu.VMEM((2, 4, NZ, ROWS, 128), BF),
            pltpu.VMEM((4, 32, ROWS, 128), BF),
            pltpu.VMEM((2, 4, 4, 4, ROWS, 128), BF),
            pltpu.VMEM((2, 4, 4, 4, ROWS, 128), BF),
            pltpu.VMEM((2, 4, NZ, ROWS, 128), BF),
            pltpu.VMEM((2, 4, NZ, ROWS, 128), BF),
            pltpu.VMEM((2, 4, NZ, ROWS, 128), BF),
            pltpu.VMEM((3, 1024, 128), F32),
            pltpu.VMEM((1024, 128), F32),
            pltpu.VMEM((8, 256, 128), F32),
            pltpu.VMEM((8, 256, 128), BF),
            pltpu.VMEM((4, 3, D, 128), BF),
            pltpu.VMEM((D, D), BF),
            pltpu.VMEM((1, D), F32),
            dma((4,)),
            dma((4, 3)),
            dma,
            pltpu.SemaphoreType.REGULAR((2, 8)),
            dma((2,)),
            dma((2, NZ)),
        ]
        + [dma((2,))] * 4
        + [dma((2, 4)), dma((2, 4)), dma((4,)), dma((2, 4)), dma((2, 4)), dma((2, 4))],
        compiler_params=pltpu.CompilerParams(
            collective_id=0, has_side_effects=True, vmem_limit_bytes=48 * 1024 * 1024
        ),
        name="axial",
    )(*(pltpu.with_memory_space_constraint(a, pltpu.HBM) for a in operands))
    return result.reshape(shape)


def solution(mesh):
    placed = (P(None, None, "gx", "gy", None), P(), P(), P())
    return jax.shard_map(
        body, mesh=mesh, in_specs=placed, out_specs=P(None, None, "gx", "gy", None), check_vma=False
    )
```

```python
import jax
import jax.numpy as jnp
from jax import lax
from jax.experimental import pallas as pl
from jax.experimental.pallas import tpu as pltpu
from jax.sharding import PartitionSpec as P

NZ = 16
ROWS = 32
D = 512
MESH = pl.DeviceIdType.MESH
BF = jnp.bfloat16
F32 = jnp.float32


def device(y, zl, core, x, zh):
    return ((y * 4 + zl) * 2 + core, x * 4 + zh)


def kernel(
    tok, gain, wq, wo, out,
    t_s, xn, r1, ry, rx, oy, ox, by, bx, sm, h, tm, qkv, of, sc, wt, w, wos, gains,
    load_sem, w_sem, loc_sem, near_sem, zs, zr, ys, yr, xs, xr, bys, byr, bxs, bxr, rs, rr,
):
    gx, gy = lax.axis_index("gx"), lax.axis_index("gy")
    y, zl, core = gx // 8, (gx // 2) % 4, gx % 2
    x, zh = gy // 4, gy % 4
    z = zh * 4 + zl
    yc = y * 2 + core

    gain_load = pltpu.make_async_copy(gain, gains, load_sem.at[3])
    gain_load.start()
    for b in range(2):
        pltpu.make_async_copy(tok.at[b], t_s.at[b], load_sem.at[b]).start()

    barrier = pltpu.get_barrier_semaphore()

    def z_peer(i):
        other = (z + (i % 2) * ((i + 1) // 2) + (1 - i % 2) * (NZ - i // 2)) % NZ
        return other, device(y, other % 4, core, x, other // 4)

    def x_peer(i):
        other = (x + i) % 4
        return other, device(y, zl, core, other, zh)

    def yc_peer(i):
        other = (yc + i) % 8
        return other, device(other // 2, zl, other % 2, x, zh)

    def each(first, last, step):
        def run(i, carry):
            step(i)
            return carry

        lax.fori_loop(first, last, run, 0)

    def greet(peer):
        return lambda i: pl.semaphore_signal(barrier, inc=1, device_id=peer(i)[1], device_id_type=MESH)

    each(1, 3, greet(z_peer))
    each(1, 4, greet(x_peer))
    each(1, 8, greet(yc_peer))

    def weight_load(pair, kind):
        cols = pl.ds(pl.multiple_of(kind * D + pair * 128, 128), 128)
        return pltpu.make_async_copy(wq.at[:, cols], w.at[pair, kind], w_sem.at[pair, kind])

    out_load = pltpu.make_async_copy(wo, wos, load_sem.at[2])
    for pair in range(4):
        for kind in range(3):
            weight_load(pair, kind).start()
    out_load.start()

    def normalize(b):
        def step(i):
            two = pl.ds(i * 2, 2)
            field = t_s[b, two].astype(F32)
            mean = jnp.mean(field * field, axis=-1, keepdims=True)
            xn[b, two] = (field * lax.rsqrt(mean + 1e-05) * gains[...]).astype(BF)

        each(0, NZ // 2, step)

    def send(src, dst, ssem, rsem, peer):
        pltpu.make_async_remote_copy(
            src_ref=src, dst_ref=dst, send_sem=ssem, recv_sem=rsem, device_id=peer, device_id_type=MESH
        ).start()

    def keep(src, dst):
        copy = pltpu.make_async_copy(src, dst, loc_sem)
        copy.start()
        copy.wait()

    def arrived(ref, sem):
        pltpu.make_async_copy(ref, ref, sem).wait()

    def forward_to(b, i):
        other, peer = z_peer(i)
        send(xn.at[b, other], r1.at[b, z], zs.at[b], zr.at[b, z], peer)

    def tell(level):
        for side in range(2):
            pl.semaphore_signal(near_sem.at[side, level], inc=1, device_id=z_peer(side + 1)[1], device_id_type=MESH)

    def forward_first():
        def step(level):
            tell(level)
            forward_to(0, 2 * level - 1)
            forward_to(0, 2 * level)
            for side in range(2):
                pl.semaphore_wait(near_sem.at[side, level], 1)

        each(1, 8, step)
        forward_to(0, 15)
        keep(xn.at[0, z], r1.at[0, z])

    def forward_second():
        each(1, NZ, lambda i: forward_to(1, i))
        keep(xn.at[1, z], r1.at[1, z])

    def spread(b):
        def pass_on(other):
            high, low_part = other // 4, other % 4
            block = r1.at[b, other]

            @pl.when((high != y) | (core != b))
            def _():
                send(block, rx.at[yc, low_part], xs.at[b], xr.at[b], device(high, zl, b, x, zh))

            @pl.when(low_part != x)
            def _():
                send(block, ry.at[b, x, high], ys.at[b], yr.at[b], device(y, zl, core, low_part, zh))

            @pl.when((high == y) & (core == b))
            def _():
                keep(block, rx.at[yc, low_part])

            @pl.when(low_part == x)
            def _():
                keep(block, ry.at[b, x, high])

        def step(i):
            other, _ = z_peer(i)
            arrived(r1.at[b, other], zr.at[b, other])
            pass_on(other)

        pass_on(z)
        each(1, NZ, step)

    def project(src, pair, tiles):
        weights = jnp.concatenate([w[pair, kind] for kind in range(3)], axis=1)

        def step(i):
            rows = pl.ds(pl.multiple_of(i * 512, 512), 512)
            part = jnp.dot(src[pl.ds(i * 16, 16)].reshape(512, D), weights, preferred_element_type=F32)
            for kind in range(3):
                qkv[kind, rows] = part[:, 128 * kind : 128 * kind + 128]

        if tiles == 1:
            step(0)
        else:
            each(0, tiles, step)

    low = lax.broadcasted_iota(jnp.int32, (128, 128), 1) < 64
    ones = jnp.ones((128, 128), BF)

    def lines(units, mask):
        def first(slot, load, store):
            q = load(0) * 0.125
            k = load(1).astype(BF)
            both = jnp.concatenate([jnp.where(low, q, 0.0), jnp.where(low, 0.0, q)], axis=0).astype(BF)
            scores = lax.dot_general(both, k, (((1,), (1,)), ((), ())), preferred_element_type=F32)
            if mask is not None:
                scores = jnp.where(mask, scores, -3e38)
            sc[slot] = scores

        def second(slot, load, store):
            scores = sc[slot]
            wt[slot] = jnp.exp(scores - jnp.max(scores, axis=-1, keepdims=True)).astype(BF)

        def third(slot, load, store):
            v = load(2).astype(BF)
            total = jnp.dot(wt[slot], jnp.concatenate([v, ones], axis=1), preferred_element_type=F32)
            part = jnp.where(low, total[:128, :128], total[128:, :128])
            norm = jnp.where(low, total[:128, 128:], total[128:, 128:])
            store(part / norm)

        for u in range(len(units) + 2):
            if u < len(units):
                first(u, *units[u])
            if 1 <= u <= len(units):
                second(u - 1, *units[u - 1])
            if u >= 2:
                third(u - 2, *units[u - 2])

    def aligned(c):
        def rows(g):
            return pl.ds(g * ROWS + c * 8, 8)

        def load(kind):
            return jnp.concatenate([qkv[kind, rows(g)] for g in range(16)], axis=0)

        def store(value):
            for g in range(16):
                of[rows(g)] = value[8 * g : 8 * g + 8]

        return load, store

    def strided(c):
        def load(kind):
            return qkv[kind, pl.ds(c, 128, stride=8)]

        def store(value):
            of[pl.ds(c, 128, stride=8)] = value

        return load, store

    def rounded(dst, blocks):
        def step(i):
            rows = pl.ds(pl.multiple_of(i * 256, 256), 256)
            dst[pl.ds(i * 8, 8)] = of[rows].reshape(8, ROWS, 128).astype(BF)

        each(0, blocks // 8, step)

    row = lax.broadcasted_iota(jnp.int32, (256, 128), 0)
    column = lax.broadcasted_iota(jnp.int32, (256, 128), 1)
    same_cell = (row % 8) == (column % 8)

    def time_lines(b):
        def step(pair):
            project(xn.at[b], pair, 1)
            lines([aligned(c) for c in range(4)], same_cell)
            rounded(tm.at[b, pair], 16)

        each(0, 4, step)

    def attend(b):
        arrived(ry.at[b, pl.ds(0, 3)], yr.at[b])

        @pl.when(core == b)
        def _():
            arrived(rx.at[pl.ds(0, 7)], xr.at[b])

        def step(pair):
            @pl.when(core == b)
            def _():
                project(rx_rows, pair, 2)
                lines([strided(c) for c in range(8)], None)
                rounded(ox.at[pair], 32)

                def give(i):
                    other, peer = yc_peer(i)
                    send(ox.at[pair, pl.ds(other * 4, 4)], bx.at[b, pair, y], bxs.at[pair], bxr.at[b, pair], peer)

                each(1, 8, give)
                keep(ox.at[pair, pl.ds(yc * 4, 4)], bx.at[b, pair, y])

            project(ry_rows.at[b], pair, 1)
            lines([aligned(c) for c in range(4)], None)
            rounded(oy.at[b, pair], 16)

            def give(i):
                other, peer = x_peer(i)
                send(oy.at[b, pair, pl.ds(other * 4, 4)], by.at[b, pair, x], bys.at[b, pair], byr.at[b, pair], peer)

            each(1, 4, give)
            keep(oy.at[b, pair, pl.ds(x * 4, 4)], by.at[b, pair, x])

            @pl.when(pair >= 1)
            def _():
                back(b, pair - 1)

        each(0, 4, step)
        back(b, 3)

    rx_rows = rx.reshape(32, ROWS, D)
    ry_rows = ry.reshape(2, 16, ROWS, D)

    def back(b, pair):
        arrived(by.at[b, pair, pl.ds(0, 3)], byr.at[b, pair])

        @pl.when(core == b)
        def _():
            arrived(bx.at[b, pair, pl.ds(0, 3)], bxr.at[b, pair])

        @pl.when(core != b)
        def _():
            arrived(bx.at[b, pair], bxr.at[b, pair])

        for high in range(4):
            for part in range(4):
                total = bx[b, pair, high, part].astype(F32) + by[b, pair, part, high].astype(F32)
                sm[b, pair, 4 * high + part] = total.astype(BF)

        def give(i):
            other, peer = z_peer(NZ - i)
            send(sm.at[b, pair, other], h.at[b, pair, z], rs.at[b, pair], rr.at[b, pair], peer)

        each(1, NZ, give)
        keep(sm.at[b, pair, z], h.at[b, pair, z])


    def finish(b):
        each(0, 4, lambda pair: arrived(h.at[b, pair, pl.ds(0, NZ - 1)], rr.at[b, pair]))

        def step(i):
            four = pl.ds(i * 4, 4)
            mixed = jnp.concatenate(
                [
                    (tm[b, pair, four].astype(F32) + h[b, pair, four].astype(F32)).reshape(128, 128)
                    for pair in range(4)
                ],
                axis=1,
            ).astype(BF)
            update = jnp.dot(mixed, wos[...], preferred_element_type=F32)
            out[b, four] = (t_s[b, four].astype(F32) + update.reshape(4, ROWS, D)).astype(BF)

        each(0, 4, step)

    pltpu.make_async_copy(tok.at[0], t_s.at[0], load_sem.at[0]).wait()
    gain_load.wait()
    normalize(0)
    pl.semaphore_wait(barrier, 12)
    forward_first()
    pltpu.make_async_copy(tok.at[1], t_s.at[1], load_sem.at[1]).wait()
    normalize(1)
    for pair in range(4):
        for kind in range(3):
            weight_load(pair, kind).wait()
    time_lines(0)
    time_lines(1)
    forward_second()
    for b in range(2):
        spread(b)
        attend(b)
    out_load.wait()
    finish(0)
    finish(1)
    for b in range(2):
        arrived(xn.at[b, pl.ds(0, NZ - 1)], zs.at[b])
        arrived(ry.at[b, pl.ds(0, 3)], ys.at[b])

        @pl.when(core == b)
        def _():
            arrived(r1.at[b, pl.ds(0, 12)], xs.at[b])
            each(0, 4, lambda pair: arrived(ox.at[pair, pl.ds(0, 28)], bxs.at[pair]))

        @pl.when(core != b)
        def _():
            arrived(r1.at[b], xs.at[b])

        def drain(pair):
            arrived(by.at[b, pair, pl.ds(0, 3)], bys.at[b, pair])
            arrived(h.at[b, pair, pl.ds(0, NZ - 1)], rs.at[b, pair])

        each(0, 4, drain)


def body(tokens, norm_gain, w_qkv, w_out):
    shape = tokens.shape
    dma = pltpu.SemaphoreType.DMA
    operands = (tokens.reshape(2, NZ, ROWS, D), norm_gain.reshape(1, D), w_qkv, w_out)
    result = pl.pallas_call(
        kernel,
        out_shape=jax.ShapeDtypeStruct((2, NZ, ROWS, D), BF),
        in_specs=[
            pl.BlockSpec(memory_space=pl.ANY),
            pl.BlockSpec(memory_space=pl.ANY),
            pl.BlockSpec(memory_space=pl.ANY),
            pl.BlockSpec(memory_space=pl.ANY),
        ],
        out_specs=pl.BlockSpec(memory_space=pltpu.VMEM),
        scratch_shapes=[
            pltpu.VMEM((2, NZ, ROWS, D), BF),
            pltpu.VMEM((2, NZ, ROWS, D), BF),
            pltpu.VMEM((2, NZ, ROWS, D), BF),
            pltpu.VMEM((2, 4, 4, ROWS, D), BF),
            pltpu.VMEM((8, 4, ROWS, D), BF),
            pltpu.VMEM((2, 4, NZ, ROWS, 128), BF),
            pltpu.VMEM((4, 32, ROWS, 128), BF),
            pltpu.VMEM((2, 4, 4, 4, ROWS, 128), BF),
            pltpu.VMEM((2, 4, 4, 4, ROWS, 128), BF),
            pltpu.VMEM((2, 4, NZ, ROWS, 128), BF),
            pltpu.VMEM((2, 4, NZ, ROWS, 128), BF),
            pltpu.VMEM((2, 4, NZ, ROWS, 128), BF),
            pltpu.VMEM((3, 1024, 128), F32),
            pltpu.VMEM((1024, 128), F32),
            pltpu.VMEM((8, 256, 128), F32),
            pltpu.VMEM((8, 256, 128), BF),
            pltpu.VMEM((4, 3, D, 128), BF),
            pltpu.VMEM((D, D), BF),
            pltpu.VMEM((1, D), F32),
            dma((4,)),
            dma((4, 3)),
            dma,
            pltpu.SemaphoreType.REGULAR((2, 8)),
            dma((2,)),
            dma((2, NZ)),
        ]
        + [dma((2,))] * 4
        + [dma((2, 4)), dma((2, 4)), dma((4,)), dma((2, 4)), dma((2, 4)), dma((2, 4))],
        compiler_params=pltpu.CompilerParams(
            collective_id=0, has_side_effects=True, vmem_limit_bytes=48 * 1024 * 1024
        ),
        name="axial",
    )(*(pltpu.with_memory_space_constraint(a, pltpu.HBM) for a in operands))
    return result.reshape(shape)


def solution(mesh):
    placed = (P(None, None, "gx", "gy", None), P(), P(), P())
    return jax.shard_map(
        body, mesh=mesh, in_specs=placed, out_specs=P(None, None, "gx", "gy", None), check_vma=False
    )
```
